32 devices in a mesh: cuts: 8 (over z, x), space: 4 (over y, core).
Axes of the slice: x: 2, y: 2, z: 4, core: 2. Of those that a mesh axis runs over, the one named last changes fastest.
Arguments:
- start_old: float32 [8, 16, 2, 2048], P('cuts', None, None, 'space'), may hold values from -3 to 3
- scales: float32 [8, 2, 2048], P('cuts', None, 'space'), may hold values from 0.92 to 1
- propagator: bfloat16 [2, 2048, 2, 2048], P(None, 'space'), may hold values from -1.2 to 1.2
- pipe_of_cell: int32 [8192], P('space'), may hold values from 0 to 127
- friction: float32 [128], replicated, may hold values from 0.02 to 0.2
Outputs:
- end_new: float32 [8, 16, 2, 2048], P('cuts', None, None, 'space')
The draws below stay inside these ranges and needn't reach their ends.
All inputs are finite; a program needn't handle non-finite values.
Results may differ from the reference program's by a relative error of at most 0.0048.
Values may be sent and summed in bfloat16 or wider, within the bound.
A program may use at most 64 MiB of HBM per device.

```python
import math
import jax
import jax.numpy as jnp
from jax import lax

NCC = 2048
REFINE = 4
STEPS = 16
NPIPE = 128
SCEN = 16
SLICES = 8
NCELL = 8192


def draw_propagator(key, part):
    matrix_order = 2 * NCC
    noise_share = 0.5
    norm_fix = 1.0 / math.sqrt(1.0 + noise_share * noise_share)
    key_perm = jax.random.fold_in(key, 11)
    key_sign = jax.random.fold_in(key, 23)
    key_noise = jax.random.fold_in(key, 37)
    target = jax.random.permutation(key_perm, matrix_order).astype(jnp.int32)
    row_signs = (2 * jax.random.randint(key_sign, (matrix_order,), 0, 2) - 1).astype(jnp.float32)
    columns = lax.broadcasted_iota(jnp.int32, (matrix_order, matrix_order), 1)
    signed_perm = jnp.where(columns == target[:, None], row_signs[:, None], 0.0).astype(jnp.float32)
    perturbation = jnp.clip(jax.random.normal(key_noise, (matrix_order, matrix_order), jnp.float32), -4.0, 4.0)
    matrix = norm_fix * (signed_perm + noise_share / math.sqrt(matrix_order) * perturbation)
    return matrix.reshape(2, NCC, 2, NCC).astype(jnp.bfloat16)


def touch_ends(array, rng, least, top_value):
    shape = array.shape
    index_at = [jax.random.randint(jax.random.fold_in(rng, axis), (), 0, shape[axis]) for axis in range(len(shape))]
    array = array.at[tuple(index_at)].set(least)
    longest = shape.index(max(shape))
    index_at[longest] = (index_at[longest] + 1) % shape[longest]
    return array.at[tuple(index_at)].set(top_value)


def block_scale(key, dims, pieces, least, high):
    def one(axis_at, shards_of):
        draws = jax.random.uniform(jax.random.fold_in(jax.random.fold_in(key, 6), axis_at), (shards_of,), jnp.float32, least / len(pieces), high / len(pieces))
        return jnp.repeat(jnp.exp(draws), dims[axis_at] // shards_of).reshape((-1,) + (1,) * (len(dims) - axis_at - 1))

    loudness = one(*pieces[0])
    for cut in pieces[1:]:
        loudness = loudness * one(*cut)
    return loudness


def bell_draw(rng, dims, deviation, bound, pieces=(), dtype=jnp.bfloat16):
    drawn = jax.random.normal(rng, dims, jnp.float32) * deviation
    if len(pieces) > 0:
        drawn = block_scale(rng, dims, pieces, -0.22, 0.18) * drawn
    return jnp.clip(drawn, min=-bound, max=bound).astype(dtype)


def setup_inputs(seed: int = 0) -> dict:
    keys = jax.random.split(jax.random.key(seed), 6)
    start_old = bell_draw(keys[0], (SLICES, SCEN, 2, NCC), 0.5, 3.0, ((0, 8), (3, 4)), jnp.float32)
    scales = jnp.clip(jnp.exp(math.log(1.0) - 0.08338159 * jax.random.uniform(keys[1], (SLICES, 2, NCC), jnp.float32) ** block_scale(keys[1], (SLICES, 2, NCC), ((0, 8), (2, 4)), -0.2, 0.2)), 0.92, 1.0)
    propagator = draw_propagator(jax.random.fold_in(keys[5], 71), 0)
    pipe_of_cell = touch_ends(jax.random.randint(keys[3], (NCELL,), 0, NPIPE), jax.random.fold_in(keys[3], 1), 0, NPIPE - 1).astype(jnp.int32)
    friction = jnp.clip(jnp.exp(jax.random.uniform(keys[4], (NPIPE,), jnp.float32, math.log(0.02), math.log(0.2))), 0.02, 0.2)
    return {"start_old": start_old, "scales": scales, "propagator": propagator, "pipe_of_cell": pipe_of_cell, "friction": friction}


def moc_step(head, flow, rate):
    hleft, hright = head[..., :-2], head[..., 2:]
    qleft, qright = flow[..., :-2], flow[..., 2:]
    plus = hleft + qleft - rate * qleft * jnp.abs(qleft)
    minus = hright - qright + rate * qright * jnp.abs(qright)
    return 0.5 * (plus + minus), 0.5 * (plus - minus)


def reference(start_old, scales, propagator, pipe_of_cell, friction):
    rate = friction[pipe_of_cell]
    field = jnp.repeat(start_old, REFINE, axis=-1)
    head, flow = field[:, :, 0, :], field[:, :, 1, :]
    widths = ((0, 0), (0, 0), (1, 1))
    for step in range(STEPS):
        head, flow = moc_step(jnp.pad(head, widths), jnp.pad(flow, widths), rate)
    fine_field = jnp.stack([head, flow], axis=2)
    fine_coarse = jnp.mean(fine_field.reshape(SLICES, SCEN, 2, NCC, REFINE), axis=-1)
    matrix = propagator.astype(jnp.float32)
    old_scaled = (scales[:, None] * start_old).astype(jnp.bfloat16)
    old_image = jnp.einsum("fiqj,nbqj->nbfi", matrix, old_scaled.astype(jnp.float32))
    delta = fine_coarse - old_image

    def advance(start, inputs):
        scale_now, delta_now = inputs
        scaled = (scale_now[None] * start).astype(jnp.bfloat16)
        ending = jnp.einsum("fiqj,bqj->bfi", matrix, scaled.astype(jnp.float32)) + delta_now
        return ending, ending

    final, end_new = lax.scan(advance, start_old[0], (scales, delta))
    return end_new
```

```python
import functools

import jax
import jax.numpy as jnp
from jax import lax
from jax.experimental import pallas as pl
from jax.experimental.pallas import tpu as pltpu
from jax.sharding import PartitionSpec as P

REFINE = 4
STEPS = 16
LANES = 128
HALF = LANES // 2
CHUNKS = 8
MESH = pl.DeviceIdType.MESH


def kernel(
    cuts, space, x_ref, scl_ref, prop_ref, pipe_ref, fric_ref, out_ref,
    raw, weight, xold, xg, dl, scl, edge, pipes, pipe8, rates,
    raw_sem, old_send, old_recv, edge_send, edge_recv, scl_send, scl_recv,
    dl_send, dl_recv, xg_send, xg_recv,
):
    c = lax.axis_index("cuts")
    s = lax.axis_index("space")
    cl = x_ref.shape[3]
    scen = x_ref.shape[1]
    width = 2 * cl
    rows = raw.shape[0] // CHUNKS
    nv = cl // LANES
    ext = cl + LANES

    raw_copies = [
        pltpu.make_async_copy(
            prop_ref.at[pl.ds(k * rows, rows)], raw.at[pl.ds(k * rows, rows)], raw_sem.at[k]
        )
        for k in range(CHUNKS)
    ]
    for copy in raw_copies:
        copy.start()

    barrier = pltpu.get_barrier_semaphore()
    for d in range(1, space):
        pl.semaphore_signal(
            barrier, inc=1, device_id={"space": lax.rem(s + d, space)}, device_id_type=MESH
        )
    for d in range(1, cuts):
        pl.semaphore_signal(
            barrier, inc=1, device_id={"cuts": lax.rem(c + d, cuts)}, device_id_type=MESH
        )

    for f in range(2):
        xold[s, :, pl.ds(f * cl, cl)] = (scl_ref[0, f, :][None] * x_ref[0, :, f, :]).astype(jnp.bfloat16)
    scl[c] = scl_ref[0]
    pl.semaphore_wait(barrier, space - 1 + cuts - 1)

    right, left = lax.rem(s + 1, space), lax.rem(s + space - 1, space)

    def remote(src, dst, send, recv, **where):
        return pltpu.make_async_remote_copy(
            src_ref=src, dst_ref=dst, send_sem=send, recv_sem=recv, device_id=where, device_id_type=MESH
        )

    edges = [
        remote(pipe_ref, pipes.at[0], edge_send.at[0], edge_recv.at[0], space=right),
        remote(pipe_ref, pipes.at[1], edge_send.at[1], edge_recv.at[1], space=left),
        remote(x_ref.at[0, :, :, pl.ds(cl - LANES, LANES)], edge.at[0], edge_send.at[2], edge_recv.at[2], space=right),
        remote(x_ref.at[0, :, :, pl.ds(0, LANES)], edge.at[1], edge_send.at[3], edge_recv.at[3], space=left),
    ]
    for copy in edges:
        copy.start()
    olds = []
    for d in range(1, space):
        peer = lax.rem(s + d, space)
        olds.append(remote(xold.at[s], xold.at[s], old_send.at[d], old_recv.at[d], space=peer))
        olds[-1].start()

    def scl_copy(slice_id, n):
        return remote(scl_ref.at[0], scl.at[slice_id], scl_send.at[n], scl_recv.at[slice_id], cuts=n)

    def dl_copy(slice_id, n):
        return remote(dl.at[slice_id], dl.at[slice_id], dl_send.at[n], dl_recv.at[slice_id], cuts=n)

    @pl.when(c > 0)
    def _():
        @pl.loop(0, cuts - 1 - c)
        def _(k):
            scl_copy(c, cuts - 1 - k).start()

    fine = REFINE * LANES
    source = lax.broadcasted_iota(jnp.int32, (fine, fine), 0)
    target = lax.broadcasted_iota(jnp.int32, (fine, fine), 1)
    pick = source == REFINE * (target % LANES) + target // LANES
    for copy in edges[:2]:
        copy.wait()
    pipe8[...] = jnp.zeros_like(pipe8)
    pipe8[pl.ds(0, nv)] = pipe_ref[...]
    pipe8[pl.ds(nv, 1)] = pipes[1, pl.ds(0, 1)]
    pipe8[pl.ds(nv + 1, 1)] = pipes[0, pl.ds(nv - 1, 1)]
    phased = jnp.dot(
        pipe8[...].astype(jnp.float32).astype(jnp.bfloat16),
        pick.astype(jnp.float32).astype(jnp.bfloat16),
        preferred_element_type=jnp.float32,
    )
    rate8 = jnp.zeros(phased.shape, jnp.float32)
    for k in range(fric_ref.shape[0]):
        rate8 = jnp.where(phased == float(k), fric_ref[k], rate8)
    near = lax.broadcasted_iota(jnp.int32, (1, LANES), 1) < HALF
    for r in range(REFINE):
        part = rate8[:, r * LANES : (r + 1) * LANES]
        for v in range(nv):
            rates[r, :, pl.ds(v * LANES, LANES)] = jnp.broadcast_to(part[v : v + 1], (scen, LANES))
        halo = jnp.where(near, part[nv : nv + 1], part[nv + 1 : nv + 2])
        rates[r, :, pl.ds(cl, LANES)] = jnp.broadcast_to(halo, (scen, LANES))

    for copy in edges[2:]:
        copy.wait()
    lane = lax.broadcasted_iota(jnp.int32, (1, ext), 1)
    has_right = (s < space - 1).astype(jnp.float32)
    has_left = (s > 0).astype(jnp.float32)
    keep = jnp.where(lane < cl, 1.0, jnp.where(lane < cl + HALF, has_right, has_left))

    def extended(f):
        halo = jnp.where(near, edge[1, :, f, :], edge[0, :, f, :])
        return keep * jnp.concatenate([x_ref[0, :, f, :], halo], axis=1)

    head, flow = extended(0), extended(1)

    def sweep(_, state):
        fwd, bwd = state
        drag = []
        for r in range(REFINE):
            q = 0.5 * (fwd[r] - bwd[r])
            drag.append(q * jnp.abs(q))
        fwd_new, bwd_new = [], []
        for r in range(REFINE):
            rate = rates[r]
            if r > 0:
                prev_f, prev_d = fwd[r - 1], drag[r - 1]
            else:
                prev_f, prev_d = pltpu.roll(fwd[-1], 1, 1), pltpu.roll(drag[-1], 1, 1)
            if r < REFINE - 1:
                next_b, next_d = bwd[r + 1], drag[r + 1]
            else:
                next_b, next_d = pltpu.roll(bwd[0], ext - 1, 1), pltpu.roll(drag[0], ext - 1, 1)
            fwd_new.append(keep * (prev_f - rate * prev_d))
            bwd_new.append(keep * (next_b + rate * next_d))
        return tuple(fwd_new), tuple(bwd_new)

    fwd, bwd = lax.fori_loop(
        0, STEPS, sweep, ((head + flow,) * REFINE, (head - flow,) * REFINE)
    )
    fwd_sum = (fwd[0] + fwd[1] + fwd[2] + fwd[3])[:, :cl]
    bwd_sum = (bwd[0] + bwd[1] + bwd[2] + bwd[3])[:, :cl]
    share = 0.5 / REFINE
    dl[c, :, pl.ds(0, cl)] = share * (fwd_sum + bwd_sum)
    dl[c, :, pl.ds(cl, cl)] = share * (fwd_sum - bwd_sum)

    def send_delta():
        @pl.loop(0, cuts - 1 - c)
        def _(k):
            dl_copy(c, cuts - 1 - k).start()

    @pl.when(c == 0)
    def _():
        send_delta()

    for k, copy in enumerate(raw_copies):
        copy.wait()
        at = pl.ds(k * rows, rows)
        for t in range(space):
            for q in range(2):
                weight[t, at, pl.ds(q * cl, cl)] = raw[at, q, pl.ds(t * cl, cl)]

    def apply_piece(piece, t):
        return lax.dot_general(
            piece, weight[t], (((1,), (1,)), ((), ())), preferred_element_type=jnp.float32
        )

    for copy in olds:
        copy.wait()

    @pl.when(c > 0)
    def _():
        image = apply_piece(xold[0], 0)
        for t in range(1, space):
            image += apply_piece(xold[t], t)
        dl[c] = dl[c] - image
        send_delta()

    def advance(m, image):
        slot = lax.rem(m, 2)
        remote(dl.at[m], dl.at[m], dl_send.at[m], dl_recv.at[m], cuts=m).wait_recv()

        @pl.when(m + 1 < c)
        def _():
            scl_copy(m + 1, m + 1).wait_recv()

        state = image + dl[m]
        for f in range(2):
            at = pl.ds(f * cl, cl)
            xg[slot, s, :, at] = (scl[m + 1, f, :][None] * state[:, f * cl : (f + 1) * cl]).astype(jnp.bfloat16)
        copies = []
        for d in range(1, space):
            peer = lax.bitwise_xor(s, d)
            copies.append(
                remote(xg.at[slot, s], xg.at[slot, s], xg_send.at[slot, d], xg_recv.at[slot, d], space=peer)
            )
            copies[-1].start()
        total = apply_piece(xg[slot, s], s)
        for d in range(1, space):
            copies[d - 1].wait_recv()
            peer = lax.bitwise_xor(s, d)
            total += apply_piece(xg[slot, peer], peer)
        for copy in copies:
            copy.wait_send()
        return total

    image = lax.fori_loop(0, c, advance, jnp.zeros((scen, width), jnp.float32))
    out_ref[...] = image + dl[c]

    @pl.loop(0, cuts - 1 - c)
    def _(k):
        dl_copy(c, cuts - 1 - k).wait_send()

    @pl.when(c > 0)
    def _():
        @pl.loop(0, cuts - 1 - c)
        def _(k):
            scl_copy(c, cuts - 1 - k).wait_send()


def solution(mesh):
    cuts, space = mesh.shape["cuts"], mesh.shape["space"]

    def local(start_old, scales, propagator, pipe_of_cell, friction):
        scen, cl = start_old.shape[1], start_old.shape[3]
        cells = propagator.shape[3]
        width = 2 * cl
        fine = REFINE * LANES
        pipes = pipe_of_cell.reshape(-1, fine)
        nv = pipes.shape[0]
        vmem = pl.BlockSpec(memory_space=pltpu.VMEM)
        dma = pltpu.SemaphoreType.DMA
        out = pl.pallas_call(
            functools.partial(kernel, cuts, space),
            out_shape=jax.ShapeDtypeStruct((scen, width), jnp.float32),
            in_specs=[vmem, vmem, pl.BlockSpec(memory_space=pl.ANY), vmem, pl.BlockSpec(memory_space=pltpu.SMEM)],
            out_specs=vmem,
            scratch_shapes=[
                pltpu.VMEM((width, 2, cells), jnp.bfloat16),
                pltpu.VMEM((space, width, width), jnp.bfloat16),
                pltpu.VMEM((space, scen, width), jnp.bfloat16),
                pltpu.VMEM((2, space, scen, width), jnp.bfloat16),
                pltpu.VMEM((cuts, scen, width), jnp.float32),
                pltpu.VMEM((cuts, 2, cl), jnp.float32),
                pltpu.VMEM((2, scen, 2, LANES), jnp.float32),
                pltpu.VMEM((2, nv, fine), jnp.int32),
                pltpu.VMEM((8, fine), jnp.int32),
                pltpu.VMEM((REFINE, scen, cl + LANES), jnp.float32),
                dma((CHUNKS,)),
                dma((space,)), dma((space,)),
                dma((4,)), dma((4,)),
                dma((cuts,)), dma((cuts,)),
                dma((cuts,)), dma((cuts,)),
                dma((2, space)), dma((2, space)),
            ],
            compiler_params=pltpu.CompilerParams(
                collective_id=0, has_side_effects=True, vmem_limit_bytes=48 * 2**20
            ),
        )(start_old, scales, propagator.reshape(width, 2, cells), pipes, friction)
        return out.reshape(1, scen, 2, cl)

    placed = (
        P("cuts", None, None, "space"),
        P("cuts", None, "space"),
        P(None, "space", None, None),
        P("space"),
        P(),
    )
    return jax.shard_map(
        local, mesh=mesh, in_specs=placed, out_specs=P("cuts", None, None, "space"), check_vma=False
    )
```

```python
import functools

import jax
import jax.numpy as jnp
from jax import lax
from jax.experimental import pallas as pl
from jax.experimental.pallas import tpu as pltpu
from jax.sharding import PartitionSpec as P

REFINE = 4
STEPS = 16
LANES = 128
HALF = LANES // 2
ROWS = 128
MESH = pl.DeviceIdType.MESH


def kernel(
    cuts, space, x_ref, scl_ref, prop_ref, pipe_ref, fric_ref, out_ref,
    raw, weight, xold, xg, dl, scl, edge, pipes, pipe8, rates,
    raw_sem, old_send, old_recv, edge_send, edge_recv, scl_send, scl_recv,
    dl_send, dl_recv, xg_send, xg_recv,
):
    c = lax.axis_index("cuts")
    s = lax.axis_index("space")
    cl = x_ref.shape[3]
    scen = x_ref.shape[1]
    width = 2 * cl
    nv = cl // LANES
    ext = cl + LANES

    def raw_copy(k):
        at = pl.ds(pl.multiple_of(k * ROWS, ROWS), ROWS)
        return pltpu.make_async_copy(prop_ref.at[at], raw.at[at], raw_sem.at[k])

    for k in range(raw.shape[0] // ROWS):
        raw_copy(k).start()

    barrier = pltpu.get_barrier_semaphore()
    for d in range(1, space):
        pl.semaphore_signal(
            barrier, inc=1, device_id={"space": lax.rem(s + d, space)}, device_id_type=MESH
        )
    for d in range(1, cuts):
        pl.semaphore_signal(
            barrier, inc=1, device_id={"cuts": lax.rem(c + d, cuts)}, device_id_type=MESH
        )

    for f in range(2):
        xold[s, :, pl.ds(f * cl, cl)] = (scl_ref[0, f, :][None] * x_ref[0, :, f, :]).astype(jnp.bfloat16)
    scl[c] = scl_ref[0]
    pl.semaphore_wait(barrier, space - 1 + cuts - 1)

    right, left = lax.rem(s + 1, space), lax.rem(s + space - 1, space)

    def remote(src, dst, send, recv, **where):
        return pltpu.make_async_remote_copy(
            src_ref=src, dst_ref=dst, send_sem=send, recv_sem=recv, device_id=where, device_id_type=MESH
        )

    edges = [
        remote(pipe_ref, pipes.at[0], edge_send.at[0], edge_recv.at[0], space=right),
        remote(pipe_ref, pipes.at[1], edge_send.at[1], edge_recv.at[1], space=left),
        remote(x_ref.at[0, :, :, pl.ds(cl - LANES, LANES)], edge.at[0], edge_send.at[2], edge_recv.at[2], space=right),
        remote(x_ref.at[0, :, :, pl.ds(0, LANES)], edge.at[1], edge_send.at[3], edge_recv.at[3], space=left),
    ]
    for copy in edges:
        copy.start()
    olds = []
    for d in range(1, space):
        peer = lax.rem(s + d, space)
        olds.append(remote(xold.at[s], xold.at[s], old_send.at[d], old_recv.at[d], space=peer))
        olds[-1].start()

    def scl_copy(slice_id, n):
        return remote(scl_ref.at[0], scl.at[slice_id], scl_send.at[n], scl_recv.at[slice_id], cuts=n)

    def dl_copy(slice_id, n):
        return remote(dl.at[slice_id], dl.at[slice_id], dl_send.at[n], dl_recv.at[slice_id], cuts=n)

    @pl.when(c > 0)
    def _():
        @pl.loop(0, cuts - 1 - c)
        def _(k):
            scl_copy(c, cuts - 1 - k).start()

    fine = REFINE * LANES
    source = lax.broadcasted_iota(jnp.int32, (fine, fine), 0)
    target = lax.broadcasted_iota(jnp.int32, (fine, fine), 1)
    pick = source == REFINE * (target % LANES) + target // LANES
    for copy in edges[:2]:
        copy.wait()
    pipe8[...] = jnp.zeros_like(pipe8)
    pipe8[pl.ds(0, nv)] = pipe_ref[...]
    pipe8[pl.ds(nv, 1)] = pipes[1, pl.ds(0, 1)]
    pipe8[pl.ds(nv + 1, 1)] = pipes[0, pl.ds(nv - 1, 1)]
    phased = jnp.dot(
        pipe8[...].astype(jnp.float32).astype(jnp.bfloat16),
        pick.astype(jnp.float32).astype(jnp.bfloat16),
        preferred_element_type=jnp.float32,
    )
    rate8 = jnp.zeros(phased.shape, jnp.float32)
    for k in range(fric_ref.shape[0]):
        rate8 = jnp.where(phased == float(k), fric_ref[k], rate8)
    near = lax.broadcasted_iota(jnp.int32, (1, LANES), 1) < HALF
    for r in range(REFINE):
        part = rate8[:, r * LANES : (r + 1) * LANES]
        for v in range(nv):
            rates[r, :, pl.ds(v * LANES, LANES)] = jnp.broadcast_to(part[v : v + 1], (scen, LANES))
        halo = jnp.where(near, part[nv : nv + 1], part[nv + 1 : nv + 2])
        rates[r, :, pl.ds(cl, LANES)] = jnp.broadcast_to(halo, (scen, LANES))

    for copy in edges[2:]:
        copy.wait()
    lane = lax.broadcasted_iota(jnp.int32, (1, ext), 1)
    has_right = (s < space - 1).astype(jnp.float32)
    has_left = (s > 0).astype(jnp.float32)
    keep = jnp.where(lane < cl, 1.0, jnp.where(lane < cl + HALF, has_right, has_left))

    def extended(f):
        halo = jnp.where(near, edge[1, :, f, :], edge[0, :, f, :])
        return keep * jnp.concatenate([x_ref[0, :, f, :], halo], axis=1)

    head, flow = extended(0), extended(1)

    def sweep(_, state):
        fwd, bwd = state
        drag = []
        for r in range(REFINE):
            q = 0.5 * (fwd[r] - bwd[r])
            drag.append(q * jnp.abs(q))
        fwd_new, bwd_new = [], []
        for r in range(REFINE):
            rate = rates[r]
            if r > 0:
                prev_f, prev_d = fwd[r - 1], drag[r - 1]
            else:
                prev_f, prev_d = pltpu.roll(fwd[-1], 1, 1), pltpu.roll(drag[-1], 1, 1)
            if r < REFINE - 1:
                next_b, next_d = bwd[r + 1], drag[r + 1]
            else:
                next_b, next_d = pltpu.roll(bwd[0], ext - 1, 1), pltpu.roll(drag[0], ext - 1, 1)
            fwd_new.append(keep * (prev_f - rate * prev_d))
            bwd_new.append(keep * (next_b + rate * next_d))
        return tuple(fwd_new), tuple(bwd_new)

    fwd, bwd = lax.fori_loop(
        0, STEPS, sweep, ((head + flow,) * REFINE, (head - flow,) * REFINE), unroll=True
    )
    fwd_sum = (fwd[0] + fwd[1] + fwd[2] + fwd[3])[:, :cl]
    bwd_sum = (bwd[0] + bwd[1] + bwd[2] + bwd[3])[:, :cl]
    share = 0.5 / REFINE
    dl[c, :, pl.ds(0, cl)] = share * (fwd_sum + bwd_sum)
    dl[c, :, pl.ds(cl, cl)] = share * (fwd_sum - bwd_sum)

    def send_delta():
        @pl.loop(0, cuts - 1 - c)
        def _(k):
            dl_copy(c, cuts - 1 - k).start()

    @pl.when(c == 0)
    def _():
        send_delta()

    @pl.loop(0, raw.shape[0] // ROWS)
    def _(k):
        at = pl.ds(pl.multiple_of(k * ROWS, ROWS), ROWS)
        raw_copy(k).wait()
        fields = pltpu.einshape("rqj->qrj", raw[at])
        for q in range(2):
            for t in range(space):
                weight[t, pl.ds(q * cl, cl), at] = fields[q][:, t * cl : (t + 1) * cl].T

    def apply_piece(piece, t):
        return lax.dot_general(
            piece, weight[t], (((1,), (0,)), ((), ())), preferred_element_type=jnp.float32
        )

    for copy in olds:
        copy.wait()

    @pl.when(c > 0)
    def _():
        image = apply_piece(xold[0], 0)
        for t in range(1, space):
            image += apply_piece(xold[t], t)
        dl[c] = dl[c] - image
        send_delta()

    def advance(m, image):
        slot = lax.rem(m, 2)
        remote(dl.at[m], dl.at[m], dl_send.at[m], dl_recv.at[m], cuts=m).wait_recv()

        @pl.when(m + 1 < c)
        def _():
            scl_copy(m + 1, m + 1).wait_recv()

        state = image + dl[m]
        for f in range(2):
            at = pl.ds(f * cl, cl)
            xg[slot, s, :, at] = (scl[m + 1, f, :][None] * state[:, f * cl : (f + 1) * cl]).astype(jnp.bfloat16)
        copies = []
        for d in range(1, space):
            peer = lax.bitwise_xor(s, d)
            copies.append(
                remote(xg.at[slot, s], xg.at[slot, s], xg_send.at[slot, d], xg_recv.at[slot, d], space=peer)
            )
            copies[-1].start()
        total = apply_piece(xg[slot, s], s)
        for d in range(1, space):
            copies[d - 1].wait_recv()
            peer = lax.bitwise_xor(s, d)
            total += apply_piece(xg[slot, peer], peer)
        for copy in copies:
            copy.wait_send()
        return total

    image = lax.fori_loop(0, c, advance, jnp.zeros((scen, width), jnp.float32))
    out_ref[...] = image + dl[c]

    @pl.loop(0, cuts - 1 - c)
    def _(k):
        dl_copy(c, cuts - 1 - k).wait_send()

    @pl.when(c > 0)
    def _():
        @pl.loop(0, cuts - 1 - c)
        def _(k):
            scl_copy(c, cuts - 1 - k).wait_send()


def solution(mesh):
    cuts, space = mesh.shape["cuts"], mesh.shape["space"]

    def local(start_old, scales, propagator, pipe_of_cell, friction):
        scen, cl = start_old.shape[1], start_old.shape[3]
        cells = propagator.shape[3]
        width = 2 * cl
        fine = REFINE * LANES
        pipes = pipe_of_cell.reshape(-1, fine)
        nv = pipes.shape[0]
        vmem = pl.BlockSpec(memory_space=pltpu.VMEM)
        dma = pltpu.SemaphoreType.DMA
        out = pl.pallas_call(
            functools.partial(kernel, cuts, space),
            out_shape=jax.ShapeDtypeStruct((scen, width), jnp.float32),
            in_specs=[vmem, vmem, pl.BlockSpec(memory_space=pl.ANY), vmem, pl.BlockSpec(memory_space=pltpu.SMEM)],
            out_specs=vmem,
            scratch_shapes=[
                pltpu.VMEM((width, 2, cells), jnp.bfloat16),
                pltpu.VMEM((space, width, width), jnp.bfloat16),
                pltpu.VMEM((space, scen, width), jnp.bfloat16),
                pltpu.VMEM((2, space, scen, width), jnp.bfloat16),
                pltpu.VMEM((cuts, scen, width), jnp.float32),
                pltpu.VMEM((cuts, 2, cl), jnp.float32),
                pltpu.VMEM((2, scen, 2, LANES), jnp.float32),
                pltpu.VMEM((2, nv, fine), jnp.int32),
                pltpu.VMEM((8, fine), jnp.int32),
                pltpu.VMEM((REFINE, scen, cl + LANES), jnp.float32),
                dma((width // ROWS,)),
                dma((space,)), dma((space,)),
                dma((4,)), dma((4,)),
                dma((cuts,)), dma((cuts,)),
                dma((cuts,)), dma((cuts,)),
                dma((2, space)), dma((2, space)),
            ],
            compiler_params=pltpu.CompilerParams(
                collective_id=0, has_side_effects=True, vmem_limit_bytes=48 * 2**20
            ),
        )(start_old, scales, propagator.reshape(width, 2, cells), pipes, friction)
        return out.reshape(1, scen, 2, cl)

    placed = (
        P("cuts", None, None, "space"),
        P("cuts", None, "space"),
        P(None, "space", None, None),
        P("space"),
        P(),
    )
    return jax.shard_map(
        local, mesh=mesh, in_specs=placed, out_specs=P("cuts", None, None, "space"), check_vma=False
    )
```

```python
import functools
import math

import jax
import jax.numpy as jnp
from jax import lax
from jax.experimental import pallas as pl
from jax.experimental.pallas import tpu as pltpu
from jax.sharding import PartitionSpec as P

REFINE = 4
STEPS = 16
LANES = 128
HALF = LANES // 2
ROWS = 128
MESH = pl.DeviceIdType.MESH


def kernel(
    cuts, space, x_ref, scl_ref, prop_ref, pipe_ref, fric_ref, out_ref,
    raw, weight, xold, xg, own, dl, res_out, res_in, scl, edge, pipes, pipe8, rates,
    raw_sem, old_send, old_recv, edge_send, edge_recv, scl_send, scl_recv,
    dl_send, dl_recv, xg_send, xg_recv, res_send, res_recv,
):
    c = lax.axis_index("cuts")
    s = lax.axis_index("space")
    cl = x_ref.shape[3]
    scen = x_ref.shape[1]
    width = 2 * cl
    nv = cl // LANES
    ext = cl + LANES
    parts, share_rows = own.shape[0], own.shape[1]
    part, rep, reps = lax.rem(c, parts), lax.div(c, parts), cuts // parts

    def raw_copy(k):
        at = pl.ds(pl.multiple_of(k * ROWS, ROWS), ROWS)
        return pltpu.make_async_copy(prop_ref.at[at], raw.at[at], raw_sem.at[k])

    for k in range(raw.shape[0] // ROWS):
        raw_copy(k).start()

    barrier = pltpu.get_barrier_semaphore()
    for d in range(1, space):
        pl.semaphore_signal(
            barrier, inc=1, device_id={"space": lax.rem(s + d, space)}, device_id_type=MESH
        )
    for d in range(1, cuts):
        pl.semaphore_signal(
            barrier, inc=1, device_id={"cuts": lax.rem(c + d, cuts)}, device_id_type=MESH
        )

    for f in range(2):
        xold[s, :, pl.ds(f * cl, cl)] = (scl_ref[0, f, :][None] * x_ref[0, :, f, :]).astype(jnp.bfloat16)
    scl[c] = scl_ref[0]
    pl.semaphore_wait(barrier, space - 1 + cuts - 1)

    right, left = lax.rem(s + 1, space), lax.rem(s + space - 1, space)

    def remote(src, dst, send, recv, **where):
        return pltpu.make_async_remote_copy(
            src_ref=src, dst_ref=dst, send_sem=send, recv_sem=recv, device_id=where, device_id_type=MESH
        )

    edges = [
        remote(pipe_ref, pipes.at[0], edge_send.at[0], edge_recv.at[0], space=right),
        remote(pipe_ref, pipes.at[1], edge_send.at[1], edge_recv.at[1], space=left),
        remote(x_ref.at[0, :, :, pl.ds(cl - LANES, LANES)], edge.at[0], edge_send.at[2], edge_recv.at[2], space=right),
        remote(x_ref.at[0, :, :, pl.ds(0, LANES)], edge.at[1], edge_send.at[3], edge_recv.at[3], space=left),
    ]
    for copy in edges:
        copy.start()
    olds = []
    for d in range(1, space):
        peer = lax.rem(s + d, space)
        olds.append(remote(xold.at[s], xold.at[s], old_send.at[d], old_recv.at[d], space=peer))
        olds[-1].start()

    def scl_copy(slice_id, n):
        return remote(scl_ref.at[0], scl.at[slice_id], scl_send.at[n], scl_recv.at[slice_id], cuts=n)

    def dl_copy(slice_id, n):
        return remote(own.at[lax.rem(n, parts)], dl.at[slice_id], dl_send.at[n], dl_recv.at[slice_id], cuts=n)

    def res_copy(n):
        return remote(res_out.at[n], res_in.at[part], res_send.at[n], res_recv.at[part], cuts=n)

    def other(k):
        return lax.rem(c + cuts - 1 - k, cuts)

    @pl.when(c > 0)
    def _():
        @pl.loop(0, cuts - 1)
        def _(k):
            scl_copy(c, other(k)).start()

    fine = REFINE * LANES
    source = lax.broadcasted_iota(jnp.int32, (fine, fine), 0)
    target = lax.broadcasted_iota(jnp.int32, (fine, fine), 1)
    pick = source == REFINE * (target % LANES) + target // LANES
    for copy in edges[:2]:
        copy.wait()
    pipe8[...] = jnp.zeros_like(pipe8)
    pipe8[pl.ds(0, nv)] = pipe_ref[...]
    pipe8[pl.ds(nv, 1)] = pipes[1, pl.ds(0, 1)]
    pipe8[pl.ds(nv + 1, 1)] = pipes[0, pl.ds(nv - 1, 1)]
    phased = jnp.dot(
        pipe8[...].astype(jnp.float32).astype(jnp.bfloat16),
        pick.astype(jnp.float32).astype(jnp.bfloat16),
        preferred_element_type=jnp.float32,
    )
    rate8 = jnp.zeros(phased.shape, jnp.float32)
    for k in range(fric_ref.shape[0]):
        rate8 = jnp.where(phased == float(k), fric_ref[k], rate8)
    near = lax.broadcasted_iota(jnp.int32, (1, LANES), 1) < HALF
    for r in range(REFINE):
        block = rate8[:, r * LANES : (r + 1) * LANES]
        for v in range(nv):
            rates[r, :, pl.ds(v * LANES, LANES)] = jnp.broadcast_to(block[v : v + 1], (scen, LANES))
        halo = jnp.where(near, block[nv : nv + 1], block[nv + 1 : nv + 2])
        rates[r, :, pl.ds(cl, LANES)] = jnp.broadcast_to(halo, (scen, LANES))

    for copy in edges[2:]:
        copy.wait()
    lane = lax.broadcasted_iota(jnp.int32, (1, ext), 1)
    has_right = (s < space - 1).astype(jnp.float32)
    has_left = (s > 0).astype(jnp.float32)
    keep = jnp.where(lane < cl, 1.0, jnp.where(lane < cl + HALF, has_right, has_left))

    def extended(f):
        halo = jnp.where(near, edge[1, :, f, :], edge[0, :, f, :])
        return keep * jnp.concatenate([x_ref[0, :, f, :], halo], axis=1)

    head, flow = extended(0), extended(1)

    def sweep(_, state):
        fwd, bwd = state
        drag = []
        for r in range(REFINE):
            q = 0.5 * (fwd[r] - bwd[r])
            drag.append(q * jnp.abs(q))
        fwd_new, bwd_new = [], []
        for r in range(REFINE):
            rate = rates[r]
            if r > 0:
                prev_f, prev_d = fwd[r - 1], drag[r - 1]
            else:
                prev_f, prev_d = pltpu.roll(fwd[-1], 1, 1), pltpu.roll(drag[-1], 1, 1)
            if r < REFINE - 1:
                next_b, next_d = bwd[r + 1], drag[r + 1]
            else:
                next_b, next_d = pltpu.roll(bwd[0], ext - 1, 1), pltpu.roll(drag[0], ext - 1, 1)
            fwd_new.append(keep * (prev_f - rate * prev_d))
            bwd_new.append(keep * (next_b + rate * next_d))
        return tuple(fwd_new), tuple(bwd_new)

    fwd, bwd = lax.fori_loop(
        0, STEPS, sweep, ((head + flow,) * REFINE, (head - flow,) * REFINE), unroll=True
    )
    fwd_sum = (fwd[0] + fwd[1] + fwd[2] + fwd[3])[:, :cl]
    bwd_sum = (bwd[0] + bwd[1] + bwd[2] + bwd[3])[:, :cl]
    share = 0.5 / REFINE
    fine_coarse = jnp.concatenate([share * (fwd_sum + bwd_sum), share * (fwd_sum - bwd_sum)], axis=1)

    def send_delta(delta):
        for p in range(parts):
            own[p] = delta[p * share_rows : (p + 1) * share_rows]
        dl[c] = own[part]

        @pl.loop(0, cuts - 1)
        def _(k):
            dl_copy(c, other(k)).start()

    @pl.when(c == 0)
    def _():
        send_delta(fine_coarse)

    @pl.loop(0, raw.shape[0] // ROWS)
    def _(k):
        at = pl.ds(pl.multiple_of(k * ROWS, ROWS), ROWS)
        raw_copy(k).wait()
        fields = pltpu.einshape("rqj->qrj", raw[at])
        for q in range(2):
            for t in range(space):
                weight[t, pl.ds(q * cl, cl), at] = fields[q][:, t * cl : (t + 1) * cl].T

    def apply_piece(piece, t):
        return lax.dot_general(
            piece, weight[t], (((1,), (0,)), ((), ())), preferred_element_type=jnp.float32
        )

    for copy in olds:
        copy.wait()

    @pl.when(c > 0)
    def _():
        image = apply_piece(xold[0], 0)
        for t in range(1, space):
            image += apply_piece(xold[t], t)
        send_delta(fine_coarse - image)

    def slice_end(m, image):
        @pl.when(m != c)
        def _():
            dl_copy(m, m).wait_recv()

        return image + dl[m]

    def hand_over(m, state):
        mine = jnp.logical_and(m > 0, lax.rem(m, reps) == rep)

        @pl.when(jnp.logical_and(mine, m == c))
        def _():
            res_in[part] = state

        @pl.when(jnp.logical_and(mine, m != c))
        def _():
            res_out[m] = state
            res_copy(m).start()

    def advance(m, image):
        slot = lax.rem(m, 2)

        @pl.when(m + 1 != c)
        def _():
            scl_copy(m + 1, m + 1).wait_recv()

        state = slice_end(m, image)
        for f in range(2):
            at = pl.ds(f * cl, cl)
            xg[slot, s, :, at] = (scl[m + 1, f, :][None] * state[:, f * cl : (f + 1) * cl]).astype(jnp.bfloat16)
        copies = []
        for d in reversed(range(1, space)):
            peer = lax.bitwise_xor(s, d)
            copies.append(
                remote(xg.at[slot, s], xg.at[slot, s], xg_send.at[slot, d], xg_recv.at[slot, d], space=peer)
            )
            copies[-1].start()
        hand_over(m, state)
        total = apply_piece(xg[slot, s], s)
        for d in range(1, space):
            copies[space - 1 - d].wait_recv()
            peer = lax.bitwise_xor(s, d)
            total += apply_piece(xg[slot, peer], peer)
        for copy in copies:
            copy.wait_send()
        return total

    image = lax.fori_loop(0, cuts - 1, advance, jnp.zeros((share_rows, width), jnp.float32))
    hand_over(cuts - 1, slice_end(cuts - 1, image))

    def write(source):
        for p in range(parts):
            for f in range(2):
                out_ref[pl.ds(p * share_rows, share_rows), pl.ds(f * cl, cl)] = source[p, :, pl.ds(f * cl, cl)]

    @pl.when(c == 0)
    def _():
        write(own)

    @pl.when(c > 0)
    def _():
        for p in range(parts):
            holder = lax.rem(c, reps) * parts + p

            @pl.when(holder != c)
            def _():
                remote(res_out.at[c], res_in.at[p], res_send.at[c], res_recv.at[p], cuts=holder).wait_recv()

        write(res_in)

    @pl.loop(0, cuts - 1)
    def _(k):
        n = other(k)
        dl_copy(c, n).wait_send()

        @pl.when(c > 0)
        def _():
            scl_copy(c, n).wait_send()

        @pl.when(jnp.logical_and(n > 0, lax.rem(n, reps) == rep))
        def _():
            res_copy(n).wait_send()


def solution(mesh):
    cuts, space = mesh.shape["cuts"], mesh.shape["space"]

    def local(start_old, scales, propagator, pipe_of_cell, friction):
        scen, cl = start_old.shape[1], start_old.shape[3]
        cells = propagator.shape[3]
        width = 2 * cl
        parts = math.gcd(cuts, scen)
        fine = REFINE * LANES
        pipes = pipe_of_cell.reshape(-1, fine)
        nv = pipes.shape[0]
        vmem = pl.BlockSpec(memory_space=pltpu.VMEM)
        dma = pltpu.SemaphoreType.DMA
        out = pl.pallas_call(
            functools.partial(kernel, cuts, space),
            out_shape=jax.ShapeDtypeStruct((scen, width), jnp.float32),
            in_specs=[vmem, vmem, pl.BlockSpec(memory_space=pl.ANY), vmem, pl.BlockSpec(memory_space=pltpu.SMEM)],
            out_specs=vmem,
            scratch_shapes=[
                pltpu.VMEM((width, 2, cells), jnp.bfloat16),
                pltpu.VMEM((space, width, width), jnp.bfloat16),
                pltpu.VMEM((space, scen, width), jnp.bfloat16),
                pltpu.VMEM((2, space, scen // parts, width), jnp.bfloat16),
                pltpu.VMEM((parts, scen // parts, width), jnp.float32),
                pltpu.VMEM((cuts, scen // parts, width), jnp.float32),
                pltpu.VMEM((cuts, scen // parts, width), jnp.float32),
                pltpu.VMEM((parts, scen // parts, width), jnp.float32),
                pltpu.VMEM((cuts, 2, cl), jnp.float32),
                pltpu.VMEM((2, scen, 2, LANES), jnp.float32),
                pltpu.VMEM((2, nv, fine), jnp.int32),
                pltpu.VMEM((8, fine), jnp.int32),
                pltpu.VMEM((REFINE, scen, cl + LANES), jnp.float32),
                dma((width // ROWS,)),
                dma((space,)), dma((space,)),
                dma((4,)), dma((4,)),
                dma((cuts,)), dma((cuts,)),
                dma((cuts,)), dma((cuts,)),
                dma((2, space)), dma((2, space)),
                dma((cuts,)), dma((parts,)),
            ],
            compiler_params=pltpu.CompilerParams(
                collective_id=0, has_side_effects=True, vmem_limit_bytes=48 * 2**20
            ),
        )(start_old, scales, propagator.reshape(width, 2, cells), pipes, friction)
        return out.reshape(1, scen, 2, cl)

    placed = (
        P("cuts", None, None, "space"),
        P("cuts", None, "space"),
        P(None, "space", None, None),
        P("space"),
        P(),
    )
    return jax.shard_map(
        local, mesh=mesh, in_specs=placed, out_specs=P("cuts", None, None, "space"), check_vma=False
    )
```

```python
import functools
import math

import jax
import jax.numpy as jnp
from jax import lax
from jax.experimental import pallas as pl
from jax.experimental.pallas import tpu as pltpu
from jax.sharding import PartitionSpec as P

REFINE = 4
STEPS = 16
LANES = 128
HALF = LANES // 2
ROWS = 128
MESH = pl.DeviceIdType.MESH


def kernel(
    cuts, space, x_ref, scl_ref, prop_ref, pipe_ref, fric_ref, out_ref,
    raw, weight, xold, xg, own, dl, res_out, res_in, scl, edge, pipes, pipe8, rates,
    raw_sem, old_send, old_recv, edge_send, edge_recv, scl_send, scl_recv,
    dl_send, dl_recv, xg_send, xg_recv, res_send, res_recv,
):
    c = lax.axis_index("cuts")
    s = lax.axis_index("space")
    cl = x_ref.shape[3]
    scen = x_ref.shape[1]
    width = 2 * cl
    nv = cl // LANES
    ext = cl + LANES
    parts, share_rows = own.shape[0], own.shape[1]
    part, rep, reps = lax.rem(c, parts), lax.div(c, parts), cuts // parts

    def raw_copy(k):
        at = pl.ds(pl.multiple_of(k * ROWS, ROWS), ROWS)
        return pltpu.make_async_copy(prop_ref.at[at], raw.at[at], raw_sem.at[k])

    for k in range(raw.shape[0] // ROWS):
        raw_copy(k).start()

    barrier = pltpu.get_barrier_semaphore()
    for d in range(1, space):
        pl.semaphore_signal(
            barrier, inc=1, device_id={"space": lax.rem(s + d, space)}, device_id_type=MESH
        )
    for d in range(1, cuts):
        pl.semaphore_signal(
            barrier, inc=1, device_id={"cuts": lax.rem(c + d, cuts)}, device_id_type=MESH
        )

    for f in range(2):
        xold[s, :, pl.ds(f * cl, cl)] = (scl_ref[0, f, :][None] * x_ref[0, :, f, :]).astype(jnp.bfloat16)
    scl[c] = scl_ref[0]
    chunks = raw.shape[0] // ROWS

    def rearrange(first, stop):
        @pl.loop(first, stop)
        def _(k):
            at = pl.ds(pl.multiple_of(k * ROWS, ROWS), ROWS)
            raw_copy(k).wait()
            fields = pltpu.einshape("rqj->qrj", raw[at])
            for q in range(2):
                for t in range(space):
                    weight[t, pl.ds(q * cl, cl), at] = fields[q][:, t * cl : (t + 1) * cl].T

    rearrange(0, chunks // 2)
    pl.semaphore_wait(barrier, space - 1 + cuts - 1)

    right, left = lax.rem(s + 1, space), lax.rem(s + space - 1, space)

    def remote(src, dst, send, recv, **where):
        return pltpu.make_async_remote_copy(
            src_ref=src, dst_ref=dst, send_sem=send, recv_sem=recv, device_id=where, device_id_type=MESH
        )

    edges = [
        remote(pipe_ref, pipes.at[0], edge_send.at[0], edge_recv.at[0], space=right),
        remote(pipe_ref, pipes.at[1], edge_send.at[1], edge_recv.at[1], space=left),
        remote(x_ref.at[0, :, :, pl.ds(cl - LANES, LANES)], edge.at[0], edge_send.at[2], edge_recv.at[2], space=right),
        remote(x_ref.at[0, :, :, pl.ds(0, LANES)], edge.at[1], edge_send.at[3], edge_recv.at[3], space=left),
    ]
    for copy in edges:
        copy.start()
    olds = []
    for d in range(1, space):
        peer = lax.rem(s + d, space)
        olds.append(remote(xold.at[s], xold.at[s], old_send.at[d], old_recv.at[d], space=peer))
        olds[-1].start()

    def scl_copy(slice_id, n):
        return remote(scl_ref.at[0], scl.at[slice_id], scl_send.at[n], scl_recv.at[slice_id], cuts=n)

    def dl_copy(slice_id, n):
        return remote(own.at[lax.rem(n, parts)], dl.at[slice_id], dl_send.at[n], dl_recv.at[slice_id], cuts=n)

    def res_copy(n):
        return remote(res_out.at[n], res_in.at[part], res_send.at[n], res_recv.at[part], cuts=n)

    def other(k):
        return lax.rem(c + cuts - 1 - k, cuts)

    @pl.when(c > 0)
    def _():
        @pl.loop(0, cuts - 1)
        def _(k):
            scl_copy(c, other(k)).start()

    rearrange(chunks // 2, chunks)

    fine = REFINE * LANES
    source = lax.broadcasted_iota(jnp.int32, (fine, fine), 0)
    target = lax.broadcasted_iota(jnp.int32, (fine, fine), 1)
    pick = source == REFINE * (target % LANES) + target // LANES
    for copy in edges[:2]:
        copy.wait()
    pipe8[...] = jnp.zeros_like(pipe8)
    pipe8[pl.ds(0, nv)] = pipe_ref[...]
    pipe8[pl.ds(nv, 1)] = pipes[1, pl.ds(0, 1)]
    pipe8[pl.ds(nv + 1, 1)] = pipes[0, pl.ds(nv - 1, 1)]
    phased = jnp.dot(
        pipe8[...].astype(jnp.float32).astype(jnp.bfloat16),
        pick.astype(jnp.float32).astype(jnp.bfloat16),
        preferred_element_type=jnp.float32,
    )
    rate8 = jnp.zeros(phased.shape, jnp.float32)
    for k in range(fric_ref.shape[0]):
        rate8 = jnp.where(phased == float(k), fric_ref[k], rate8)
    near = lax.broadcasted_iota(jnp.int32, (1, LANES), 1) < HALF
    for r in range(REFINE):
        block = rate8[:, r * LANES : (r + 1) * LANES]
        for v in range(nv):
            rates[r, :, pl.ds(v * LANES, LANES)] = jnp.broadcast_to(block[v : v + 1], (scen, LANES))
        halo = jnp.where(near, block[nv : nv + 1], block[nv + 1 : nv + 2])
        rates[r, :, pl.ds(cl, LANES)] = jnp.broadcast_to(halo, (scen, LANES))

    for copy in edges[2:]:
        copy.wait()
    lane = lax.broadcasted_iota(jnp.int32, (1, ext), 1)
    has_right = (s < space - 1).astype(jnp.float32)
    has_left = (s > 0).astype(jnp.float32)
    keep = jnp.where(lane < cl, 1.0, jnp.where(lane < cl + HALF, has_right, has_left))

    def extended(f):
        halo = jnp.where(near, edge[1, :, f, :], edge[0, :, f, :])
        return keep * jnp.concatenate([x_ref[0, :, f, :], halo], axis=1)

    head, flow = extended(0), extended(1)

    def sweep(_, state):
        fwd, bwd = state
        drag = []
        for r in range(REFINE):
            q = 0.5 * (fwd[r] - bwd[r])
            drag.append(q * jnp.abs(q))
        fwd_new, bwd_new = [], []
        for r in range(REFINE):
            rate = rates[r]
            if r > 0:
                prev_f, prev_d = fwd[r - 1], drag[r - 1]
            else:
                prev_f, prev_d = pltpu.roll(fwd[-1], 1, 1), pltpu.roll(drag[-1], 1, 1)
            if r < REFINE - 1:
                next_b, next_d = bwd[r + 1], drag[r + 1]
            else:
                next_b, next_d = pltpu.roll(bwd[0], ext - 1, 1), pltpu.roll(drag[0], ext - 1, 1)
            fwd_new.append(keep * (prev_f - rate * prev_d))
            bwd_new.append(keep * (next_b + rate * next_d))
        return tuple(fwd_new), tuple(bwd_new)

    fwd, bwd = lax.fori_loop(
        0, STEPS, sweep, ((head + flow,) * REFINE, (head - flow,) * REFINE), unroll=True
    )
    fwd_sum = (fwd[0] + fwd[1] + fwd[2] + fwd[3])[:, :cl]
    bwd_sum = (bwd[0] + bwd[1] + bwd[2] + bwd[3])[:, :cl]
    share = 0.5 / REFINE
    fine_coarse = jnp.concatenate([share * (fwd_sum + bwd_sum), share * (fwd_sum - bwd_sum)], axis=1)

    def send_delta(delta):
        for p in range(parts):
            own[p] = delta[p * share_rows : (p + 1) * share_rows]
        dl[c] = own[part]

        @pl.loop(0, cuts - 1)
        def _(k):
            dl_copy(c, other(k)).start()

    @pl.when(c == 0)
    def _():
        send_delta(fine_coarse)

    def apply_piece(piece, t):
        return lax.dot_general(
            piece, weight[t], (((1,), (0,)), ((), ())), preferred_element_type=jnp.float32
        )

    for copy in olds:
        copy.wait()

    @pl.when(c > 0)
    def _():
        image = apply_piece(xold[0], 0)
        for t in range(1, space):
            image += apply_piece(xold[t], t)
        send_delta(fine_coarse - image)

    def slice_end(m, image):
        @pl.when(m != c)
        def _():
            dl_copy(m, m).wait_recv()

        return image + dl[m]

    def hand_over(m, state):
        mine = jnp.logical_and(m > 0, lax.rem(m, reps) == rep)

        @pl.when(jnp.logical_and(mine, m == c))
        def _():
            res_in[part] = state

        @pl.when(jnp.logical_and(mine, m != c))
        def _():
            res_out[m] = state
            res_copy(m).start()

    def advance(m, image):
        slot = lax.rem(m, 2)

        @pl.when(m + 1 != c)
        def _():
            scl_copy(m + 1, m + 1).wait_recv()

        state = slice_end(m, image)
        for f in range(2):
            at = pl.ds(f * cl, cl)
            xg[slot, s, :, at] = (scl[m + 1, f, :][None] * state[:, f * cl : (f + 1) * cl]).astype(jnp.bfloat16)
        copies = []
        for d in reversed(range(1, space)):
            peer = lax.bitwise_xor(s, d)
            copies.append(
                remote(xg.at[slot, s], xg.at[slot, s], xg_send.at[slot, d], xg_recv.at[slot, d], space=peer)
            )
            copies[-1].start()
        hand_over(m, state)
        total = apply_piece(xg[slot, s], s)
        for d in range(1, space):
            copies[space - 1 - d].wait_recv()
            peer = lax.bitwise_xor(s, d)
            total += apply_piece(xg[slot, peer], peer)
        for copy in copies:
            copy.wait_send()
        return total

    image = lax.fori_loop(0, cuts - 1, advance, jnp.zeros((share_rows, width), jnp.float32))
    hand_over(cuts - 1, slice_end(cuts - 1, image))

    def write(source):
        for p in range(parts):
            for f in range(2):
                out_ref[pl.ds(p * share_rows, share_rows), pl.ds(f * cl, cl)] = source[p, :, pl.ds(f * cl, cl)]

    @pl.when(c == 0)
    def _():
        write(own)

    @pl.when(c > 0)
    def _():
        for p in range(parts):
            holder = lax.rem(c, reps) * parts + p

            @pl.when(holder != c)
            def _():
                remote(res_out.at[c], res_in.at[p], res_send.at[c], res_recv.at[p], cuts=holder).wait_recv()

        write(res_in)

    @pl.loop(0, cuts - 1)
    def _(k):
        n = other(k)
        dl_copy(c, n).wait_send()

        @pl.when(c > 0)
        def _():
            scl_copy(c, n).wait_send()

        @pl.when(jnp.logical_and(n > 0, lax.rem(n, reps) == rep))
        def _():
            res_copy(n).wait_send()


def solution(mesh):
    cuts, space = mesh.shape["cuts"], mesh.shape["space"]

    def local(start_old, scales, propagator, pipe_of_cell, friction):
        scen, cl = start_old.shape[1], start_old.shape[3]
        cells = propagator.shape[3]
        width = 2 * cl
        parts = math.gcd(cuts, scen)
        fine = REFINE * LANES
        pipes = pipe_of_cell.reshape(-1, fine)
        nv = pipes.shape[0]
        vmem = pl.BlockSpec(memory_space=pltpu.VMEM)
        dma = pltpu.SemaphoreType.DMA
        out = pl.pallas_call(
            functools.partial(kernel, cuts, space),
            out_shape=jax.ShapeDtypeStruct((scen, width), jnp.float32),
            in_specs=[vmem, vmem, pl.BlockSpec(memory_space=pl.ANY), vmem, pl.BlockSpec(memory_space=pltpu.SMEM)],
            out_specs=vmem,
            scratch_shapes=[
                pltpu.VMEM((width, 2, cells), jnp.bfloat16),
                pltpu.VMEM((space, width, width), jnp.bfloat16),
                pltpu.VMEM((space, scen, width), jnp.bfloat16),
                pltpu.VMEM((2, space, scen // parts, width), jnp.bfloat16),
                pltpu.VMEM((parts, scen // parts, width), jnp.float32),
                pltpu.VMEM((cuts, scen // parts, width), jnp.float32),
                pltpu.VMEM((cuts, scen // parts, width), jnp.float32),
                pltpu.VMEM((parts, scen // parts, width), jnp.float32),
                pltpu.VMEM((cuts, 2, cl), jnp.float32),
                pltpu.VMEM((2, scen, 2, LANES), jnp.float32),
                pltpu.VMEM((2, nv, fine), jnp.int32),
                pltpu.VMEM((8, fine), jnp.int32),
                pltpu.VMEM((REFINE, scen, cl + LANES), jnp.float32),
                dma((width // ROWS,)),
                dma((space,)), dma((space,)),
                dma((4,)), dma((4,)),
                dma((cuts,)), dma((cuts,)),
                dma((cuts,)), dma((cuts,)),
                dma((2, space)), dma((2, space)),
                dma((cuts,)), dma((parts,)),
            ],
            compiler_params=pltpu.CompilerParams(
                collective_id=0, has_side_effects=True, vmem_limit_bytes=48 * 2**20
            ),
        )(start_old, scales, propagator.reshape(width, 2, cells), pipes, friction)
        return out.reshape(1, scen, 2, cl)

    placed = (
        P("cuts", None, None, "space"),
        P("cuts", None, "space"),
        P(None, "space", None, None),
        P("space"),
        P(),
    )
    return jax.shard_map(
        local, mesh=mesh, in_specs=placed, out_specs=P("cuts", None, None, "space"), check_vma=False
    )
```
